32 devices in a mesh: day: 4 (over x, core), row: 8 (over z, y).
Axes of the slice: x: 2, y: 2, z: 4, core: 2. Of those that a mesh axis runs over, the one named last changes fastest.
Arguments:
- field: float32 [128, 1024, 1024], P('day', 'row'), may hold values from -6 to 6
- basis_day: float32 [128, 128], replicated, as said below
- basis_x: float32 [1024, 1024], replicated, as said below
- basis_y: float32 [1024, 1024], replicated, as said below
- eig_day: float32 [128], replicated, may hold values from 0.05 to 3
- eig_x: float32 [1024], replicated, may hold values from 0.05 to 3
- eig_y: float32 [1024], replicated, may hold values from 0.05 to 3
- noise: float32 [1], replicated, may hold values from 0.1 to 0.5
Outputs:
- weights: float32 [128, 1024, 1024], P('day', 'row')
The draws below stay inside these ranges and needn't reach their ends.
Inputs may be any that keep to these rules, and one draw needn't show every extreme that they name: basis_day is orthogonal. basis_x is orthogonal. basis_y is orthogonal.
All inputs are finite; a program needn't handle non-finite values.
Results may differ from the reference program's by a relative error of at most 0.00007.
Values sent between devices are 32-bit elements; how exact they have to be, the bound alone decides.
A program may use at most 128 MiB of HBM per device.

```python
import math
import jax
import jax.numpy as jnp
from jax import lax

DAYS = 128
NX = 1024
NY = 1024


def orthogonal(key, order):
    matrix = jax.random.normal(key, (order, order), jnp.float32)
    factor, upper = jnp.linalg.qr(matrix)
    return factor


def draw_basis_day(key, part):
    return orthogonal(jax.random.fold_in(key, 11), DAYS)


def draw_basis_x(key, part):
    return orthogonal(jax.random.fold_in(key, 23), NX)


def draw_basis_y(key, part):
    return orthogonal(jax.random.fold_in(key, 37), NY)


def levels(own_key, shape, cuts, low, high):
    def one(position, parts):
        draws = jax.random.uniform(jax.random.fold_in(jax.random.fold_in(own_key, 6), position), (parts,), jnp.float32, low / len(cuts), high / len(cuts))
        return jnp.repeat(jnp.exp(draws), shape[position] // parts).reshape((-1,) + (1,) * (len(shape) - position - 1))

    loudness = one(*cuts[0])
    for cut in cuts[1:]:
        loudness = loudness * one(*cut)
    return loudness


def normal_values(rng, extent, deviation, limit, pieces=(), kind=jnp.bfloat16):
    loudness = levels(rng, extent, pieces, -0.22, 0.18) if pieces else 1.0
    result = jax.random.normal(rng, extent, jnp.float32) * deviation * loudness
    return jnp.minimum(jnp.maximum(result, -limit), limit).astype(kind)


def setup_inputs(seed: int = 0) -> dict:
    key_of = jax.random.split(jax.random.key(seed), 9)
    return {
        "field": normal_values(key_of[0], (DAYS, NX, NY), 1.0, 6.0, ((0, 4), (1, 8)), jnp.float32),
        "basis_day": draw_basis_day(jax.random.fold_in(key_of[8], 71), 0),
        "basis_x": draw_basis_x(jax.random.fold_in(key_of[8], 71), 0),
        "basis_y": draw_basis_y(jax.random.fold_in(key_of[8], 71), 0),
        "eig_day": jnp.clip(jnp.exp(jax.random.uniform(key_of[4], (DAYS,), jnp.float32, math.log(0.05), math.log(3.0))), 0.05, 3.0),
        "eig_x": jnp.clip(jnp.exp(jax.random.uniform(key_of[5], (NX,), jnp.float32, math.log(0.05), math.log(3.0))), 0.05, 3.0),
        "eig_y": jnp.clip(jnp.exp(jax.random.uniform(key_of[6], (NY,), jnp.float32, math.log(0.05), math.log(3.0))), 0.05, 3.0),
        "noise": jnp.clip(jnp.exp(jax.random.uniform(key_of[7], (1,), jnp.float32, math.log(0.1), math.log(0.5))), 0.1, 0.5),
    }


def reference(field, basis_day, basis_x, basis_y, eig_day, eig_x, eig_y, noise):
    precise = lax.Precision.HIGHEST
    along_y = jnp.einsum('txy,yb->txb', field, basis_y, precision=precise)
    along_x = jnp.einsum('txb,xa->tab', along_y, basis_x, precision=precise)
    spectral = jnp.einsum('tab,ts->sab', along_x, basis_day, precision=precise)
    spectrum = eig_day[:, None, None] * eig_x[None, :, None] * eig_y[None, None, :] + noise[0]
    scaled = spectral / spectrum
    back_day = jnp.einsum('sab,ts->tab', scaled, basis_day, precision=precise)
    back_x = jnp.einsum('tab,xa->txb', back_day, basis_x, precision=precise)
    return jnp.einsum('txb,yb->txy', back_x, basis_y, precision=precise)
```

```python
import jax
import jax.numpy as jnp
from jax import lax
from jax.sharding import PartitionSpec as P

CHUNKS = 4


def shift(block, axis, step):
    size = lax.axis_size(axis)
    if step % size == 0:
        return block
    return lax.ppermute(block, axis, [(i, (i + step) % size) for i in range(size)])


def rolled(array, dim, blocks, first, sign):
    width = array.shape[dim] // blocks
    starts = [((first + sign * j) % blocks) * width for j in range(blocks)]
    return jnp.concatenate([lax.dynamic_slice_in_dim(array, start, width, dim) for start in starts], axis=dim)


def body(field, basis_day, basis_x, basis_y, eig_day, eig_x, eig_y, noise):
    precise = lax.Precision.HIGH
    days = lax.axis_size("day")
    rows = lax.axis_size("row")
    day = lax.axis_index("day")
    row = lax.axis_index("row")
    local_days, local_rows, grid_cols = field.shape
    grid_rows = basis_x.shape[0]
    own_cols = grid_cols // rows
    own_spec = grid_rows // days
    chunks = max(1, min(CHUNKS, own_cols // 32))
    width = own_cols // chunks

    def product(spec, left, right):
        return jnp.einsum(spec, left, right, precision=precise, preferred_element_type=jnp.float32)

    turn_x = rolled(rolled(basis_x, 0, rows, row, -1), 1, days, day, 1)
    turn_y = rolled(basis_y.T, 0, rows, row, 1).reshape(rows, chunks, width, grid_cols)
    turn_day = rolled(basis_day, 0, days, day, -1)
    part_x = lax.dynamic_slice_in_dim(eig_x, day * own_spec, own_spec)
    part_y = lax.dynamic_slice_in_dim(eig_y, row * own_cols, own_cols)
    parts = []
    for chunk in range(chunks):
        basis = turn_y[:, chunk].reshape(rows * width, grid_cols)
        along_y = product("by,txy->btx", basis, field)
        got = [shift(along_y[j * width : (j + 1) * width], "row", j) for j in range(rows)]
        along_x = product("btx,xa->bta", jnp.concatenate(got, axis=2), turn_x)
        got = [shift(along_x[:, :, j * own_spec : (j + 1) * own_spec], "day", j) for j in range(days)]
        spectral = product("ts,bta->bsa", turn_day, jnp.concatenate(got, axis=1))
        own_y = part_y[chunk * width : (chunk + 1) * width]
        spectrum = eig_day[None, :, None] * part_x[None, None, :] * own_y[:, None, None] + noise[0]
        back_day = product("ts,bsa->bta", turn_day, spectral / spectrum)
        got = [shift(back_day[:, j * local_days : (j + 1) * local_days], "day", -j) for j in range(days)]
        back_x = product("bta,xa->btx", jnp.concatenate(got, axis=2), turn_x)
        got = [shift(back_x[:, :, j * local_rows : (j + 1) * local_rows], "row", -j) for j in range(rows)]
        parts.append((basis, jnp.concatenate(got, axis=0)))
    weights = None
    for group in (parts[:-1], parts[-1:]):
        if group:
            basis = jnp.concatenate([g[0] for g in group], axis=0)
            value = product("btx,by->txy", jnp.concatenate([g[1] for g in group], axis=0), basis)
            weights = value if weights is None else weights + value
    return weights


def solution(mesh):
    in_specs = (P("day", "row", None), P(), P(), P(), P(), P(), P(), P())
    out_specs = P("day", "row", None)
    return jax.shard_map(body, mesh=mesh, in_specs=in_specs, out_specs=out_specs, check_vma=False)
```
